512 devices in a mesh: rowa: 16 (over y, x), rowb: 32 (over z, core).
Axes of the slice: x: 4, y: 4, z: 16, core: 2. Of those that a mesh axis runs over, the one named last changes fastest.
Arguments:
- right_side: float32 [196608, 8], P(('rowa', 'rowb')), may hold values from -6 to 6
- leaves: float32 [196608, 384], P(('rowa', 'rowb')), as said below
- bases: float32 [9, 196608, 128], P(None, ('rowa', 'rowb')), may hold values from -0.3125 to 0.3125
- ranks: int32 [511], replicated, may hold values from 64 to 128
Outputs:
- solution: float32 [196608, 8], P(('rowa', 'rowb'))
The draws below stay inside these ranges and needn't reach their ends.
Inputs may be any that keep to these rules, and one draw needn't show every extreme that they name: `ranks`: entry 2^(9 - m) + k - 1 is the rank of node k of level m (levels counted from the leaves, the root at level 9). `leaves`: each leaf block is symmetric positive definite.
All inputs are finite; a program needn't handle non-finite values.
Results may differ from the reference program's by a relative error of at most 0.0001.
Values sent between devices are 32-bit elements; how exact they have to be, the bound alone decides.
A program may use at most 64 MiB of HBM per device.

```python
import jax
import jax.numpy as jnp
from jax import lax

LEAF = 384
RMAX = 128
NRHS = 8
LEVELS = 9
NTOT = 196608
DEVICES = 512


def draw_leaves(key, part):
    key_locations = jax.random.fold_in(key, 11)
    key_shift = jax.random.fold_in(key, 12)
    block_count = NTOT // LEAF
    side = 0.5 * jnp.sqrt(jnp.float32(LEAF))
    points = jax.random.uniform(key_locations, (block_count, LEAF, 2), jnp.float32) * side
    shift = jnp.exp(jax.random.uniform(key_shift, (block_count, LEAF), jnp.float32, jnp.log(0.5), jnp.log(2.0)))
    squares = jnp.sum(points * points, axis=2)
    inner = jnp.einsum('pid,pjd->pij', points, points)
    squared_distance = squares[:, :, None] + squares[:, None, :] - 2.0 * inner
    kernel = jnp.exp(-0.5 * jnp.maximum(squared_distance, 0.0))
    kernel = 0.5 * (kernel + jnp.swapaxes(kernel, 1, 2))
    eye_block = jnp.eye(LEAF, dtype=jnp.float32)[None]
    matrix = kernel + eye_block * shift[:, :, None]
    return matrix.reshape(NTOT, LEAF)


def touch_ends(entries, rng, least, top_value):
    longest = entries.shape.index(max(entries.shape))
    spots = []
    for shift in (0, 1):
        where = [jax.random.randint(jax.random.fold_in(rng, axis), (), 0, length) for axis, length in enumerate(entries.shape)]
        where[longest] = (where[longest] + shift) % entries.shape[longest]
        spots.append(tuple(where))
    return entries.at[spots[0]].set(least).at[spots[1]].set(top_value)


def block_scale(key, shape, shards, low, top_value):
    def one(dim, blocks):
        draws = jax.random.uniform(jax.random.fold_in(jax.random.fold_in(key, 6), dim), (blocks,), jnp.float32, low / len(shards), top_value / len(shards))
        return jnp.repeat(jnp.exp(draws), shape[dim] // blocks).reshape((-1,) + (1,) * (len(shape) - dim - 1))

    factor_of = one(*shards[0])
    for cut in shards[1:]:
        factor_of = factor_of * one(*cut)
    return factor_of


def noise(rng, dims, scale, most, pieces=(), held_as=jnp.bfloat16):
    values = scale * jax.random.normal(rng, dims, jnp.float32)
    if pieces:
        values = values * block_scale(rng, dims, pieces, -0.22, 0.18)
    return jnp.clip(values, -most, most).astype(held_as)


def setup_inputs(seed: int = 0) -> dict:
    splits = jax.random.split(jax.random.key(seed), 5)
    right_side = noise(splits[0], (NTOT, NRHS), 1.0, 6.0, ((0, 512),), jnp.float32)
    leaves = draw_leaves(jax.random.fold_in(splits[4], 71), 0)
    bases = noise(splits[2], (LEVELS, NTOT, RMAX), LEAF ** -0.5, 0.3125, ((1, 512),), jnp.float32)
    ranks = touch_ends(jax.random.randint(splits[3], (DEVICES - 1,), RMAX // 2, RMAX + 1), jax.random.fold_in(splits[3], 1), RMAX // 2, RMAX).astype(jnp.int32)
    return {"right_side": right_side, "leaves": leaves, "bases": bases, "ranks": ranks}


PRECISION_HIGH = lax.Precision.HIGHEST

def factored_system_solve(factor, values):
    half = lax.linalg.triangular_solve(factor, values, left_side=True, lower=True)
    return lax.linalg.triangular_solve(factor, half, left_side=True, lower=True, transpose_a=True)

def leaf_solve(inputs):
    block, rhs_block, basis_block = inputs
    factor = jnp.linalg.cholesky(block)
    return (factored_system_solve(factor, rhs_block), factored_system_solve(factor, basis_block))

def reference(right_side, leaves, bases, ranks):
    block_count = NTOT // LEAF
    columns = jnp.arange(RMAX)
    masked_values = []
    for tree_level in range(1, LEVELS + 1):
        node_index = jnp.arange(block_count) // 2 ** tree_level
        node_rank = ranks[2 ** (LEVELS - tree_level) + node_index - 1]
        keep = (columns[None, :] < node_rank[:, None]).astype(jnp.float32)
        masked_values.append(bases[tree_level - 1].reshape(block_count, LEAF, RMAX) * keep[:, None, :])
    stacked = jnp.concatenate(masked_values, axis=2)
    blocks = leaves.reshape(block_count, LEAF, LEAF)
    solution, corrected = lax.map(leaf_solve, (blocks, right_side.reshape(block_count, LEAF, NRHS), stacked))
    for tree_level in range(1, LEVELS + 1):
        node_count = block_count // 2 ** tree_level
        covered_rows = LEAF * 2 ** tree_level
        level_basis = masked_values[tree_level - 1].reshape(node_count, covered_rows, RMAX)
        current_all = corrected.reshape(node_count, covered_rows, -1)
        current_rhs = solution.reshape(node_count, covered_rows, NRHS)
        products = jnp.einsum('qir,qic->qrc', level_basis, current_all, precision=PRECISION_HIGH)
        right_terms = jnp.einsum('qir,qic->qrc', level_basis, current_rhs, precision=PRECISION_HIGH)
        capacitance = jnp.eye(RMAX, dtype=products.dtype)[None] + products[:, :, :RMAX]
        cap_factor = jnp.linalg.cholesky(capacitance)
        current = current_all[:, :, :RMAX]
        coef_rhs = jax.vmap(factored_system_solve)(cap_factor, right_terms)
        current_rhs = current_rhs - jnp.einsum('qir,qrc->qic', current, coef_rhs, precision=PRECISION_HIGH)
        solution = current_rhs.reshape(block_count, LEAF, NRHS)
        if tree_level < LEVELS:
            coef_rest = jax.vmap(factored_system_solve)(cap_factor, products[:, :, RMAX:])
            remaining = current_all[:, :, RMAX:] - jnp.einsum('qir,qrc->qic', current, coef_rest, precision=PRECISION_HIGH)
            corrected = remaining.reshape(block_count, LEAF, -1)
    return solution.reshape(NTOT, NRHS)
```

```python
import jax
import jax.numpy as jnp
from jax import lax
from jax.experimental import pallas as pl
from jax.experimental.pallas import tpu as pltpu
from jax.sharding import PartitionSpec as P

F32 = jnp.float32
HI = lax.Precision.HIGHEST
MESH = pl.DeviceIdType.MESH
R = 128
LEAF = 384
LEVELS = 9
NZ, NX, NY = 16, 4, 4
WROWS = LEVELS * R + 16
WUSED = LEVELS * R + 8
HALF2, HALF3 = 520, 456
PART = 112
ZHALF = NZ * PART
ZROWS = 2 * ZHALF
O4 = 776
O = {5: 1552, 6: 2200, 7: 2720, 8: 3112, 9: 3376}
OEND = 3512
XROWS, YROWS = 1312, 400


def dot(a, b, ca=1, cb=0):
    return lax.dot_general(a, b, (((ca,), (cb,)), ((), ())), precision=HI, preferred_element_type=F32)


def wo(level):
    return (level - 1) * R


def rows_of(level):
    return (LEVELS + 1 - level) * R + 8


def inv128(a):
    lane = lax.broadcasted_iota(jnp.int32, (8, R), 1)
    sub = lax.broadcasted_iota(jnp.int32, (8, R), 0)
    lanes = lax.broadcasted_iota(jnp.int32, (R, R), 1)
    for lo in range(0, R, 8):
        panel = a[lo : lo + 8, :]
        small = [jnp.broadcast_to(panel[:, lo + j : lo + j + 1], (8, R)) for j in range(8)]
        wide = [jnp.broadcast_to(a[:, lo + j : lo + j + 1], (R, R)) for j in range(8)]
        inside = (lane >= lo) & (lane < lo + 8)
        rows = jnp.where(inside, jnp.where(lane - lo == sub, 1.0, 0.0), panel)
        for k in range(8):
            pivot = 1.0 / small[k][k : k + 1, :]
            here = sub == k
            column = small[k]
            line = jnp.broadcast_to(rows[k : k + 1, :] * pivot, (8, R))
            rows = jnp.where(here, line, rows - column * line)
            for j in range(k + 1, 8):
                line = jnp.broadcast_to(small[j][k : k + 1, :] * pivot, (8, R))
                small[j] = jnp.where(here, line, small[j] - column * line)
        rest = jnp.where((lanes >= lo) & (lanes < lo + 8), 0.0, a)
        for j in range(8):
            rest = rest - wide[j] * rows[j : j + 1, :]
        parts = [part for part in (rest[:lo], rows, rest[lo + 8 :]) if part.shape[0]]
        a = jnp.concatenate(parts, axis=0)
    return a


def eye():
    row = lax.broadcasted_iota(jnp.int32, (R, R), 0)
    column = lax.broadcasted_iota(jnp.int32, (R, R), 1)
    return jnp.where(row == column, 1.0, 0.0).astype(F32)


def flipped(value, mask):
    for bit in (1, 2, 4, 8):
        if mask & bit:
            value = value + bit - 2 * bit * ((value // bit) % 2)
    return value


def kernel(
    ranks, rhs, leaves, bases, out,
    zz, wt, dd, pt1, r1, pt2, a2, s2, b2, t2, pt3, a3, s3, b3, s3b, c3, t3,
    bb, rz, hh, s_r, r_r, s_l, r_l, tt, ki, xm, xb, u6, k6, s7, ym, yb,
    send_sems, recv_sems,
):
    ra, rb = lax.axis_index("rowa"), lax.axis_index("rowb")
    y, x, z, c = ra // NX, ra % NX, rb // 2, rb % 2
    position = ra * (2 * NZ) + rb

    def device(y=y, x=x, z=z, c=c):
        return (y * NX + x, z * 2 + c)

    partner = device(c=1 - c)
    above, below = device(z=(z + 1) % NZ), device(z=(z + NZ - 1) % NZ)
    z1, z2 = device(z=flipped(z, 1)), device(z=flipped(z, 2))
    xs = [device(x=flipped(x, i)) for i in (1, 2, 3)]
    ys = [device(y=flipped(y, i)) for i in (1, 2, 3)]
    met = [partner, above, below, z2] + xs + ys
    barrier = pltpu.get_barrier_semaphore()
    for other in met:
        pl.semaphore_signal(barrier, inc=1, device_id=other, device_id_type=MESH)

    used = [0]
    started = []

    def send(src, dst, to):
        at = used[0]
        used[0] += 1
        copy = pltpu.make_async_remote_copy(
            src_ref=src, dst_ref=dst, send_sem=send_sems.at[at], recv_sem=recv_sems.at[at],
            device_id=to, device_id_type=MESH,
        )
        copy.start()
        started.append(copy)
        return copy

    def sent():
        for copy in started:
            copy.wait_send()
        started.clear()

    dd[...] = leaves[...]
    for k in range(3):
        mine = pl.ds(k * R, R)
        inverse = inv128(dd[mine, mine])
        column = lax.broadcasted_iota(jnp.int32, (R, LEAF), 1) // R
        panel = jnp.where(column == k, 0.0, dd[mine, :])
        line = dot(inverse, panel)
        line = jnp.concatenate([inverse if j == k else line[:, j * R : (j + 1) * R] for j in range(3)], axis=1)
        for i in range(3):
            if i != k:
                there = pl.ds(i * R, R)
                dd[there, :] = jnp.where(column == k, 0.0, dd[there, :]) - dot(dd[there, mine], line)
        dd[mine, :] = line

    lane = lax.broadcasted_iota(jnp.int32, (LEAF, R), 1)
    for level in range(1, LEVELS + 1):
        rank = ranks[2 ** (LEVELS - level) + position // 2**level - 1]
        zz[level - 1] = jnp.where(lane < rank, bases[level - 1], 0.0)

    @pl.loop(0, LEVELS)
    def _(j):
        wt[pl.ds(pl.multiple_of(j * R, R), R), :] = dot(zz[j], dd[...], 0, 0)

    wt[pl.ds(LEVELS * R, 8), :] = dot(rhs[...], dd[...], 0, 0)
    wt[pl.ds(WUSED, 8), :] = jnp.zeros((8, LEAF), F32)

    pl.semaphore_wait(barrier, len(met))

    def eliminated(total, level):
        inverse = inv128(eye() + total[pl.ds(0, R), :])
        mine = dot(inverse, wt[pl.ds(wo(level), R), :])
        rest = pl.ds(wo(level + 1), WROWS - wo(level + 1))
        wt[rest, :] = wt[rest, :] - dot(total[pl.ds(R, WROWS - wo(level + 1)), :], mine)

    pt1[...] = dot(wt[...], zz[0])
    send(pt1, r1, partner).wait_recv()
    r1[...] = r1[...] + pt1[...]
    eliminated(r1, 1)

    own2, far2 = pl.multiple_of(c * HALF2, 8), pl.multiple_of((1 - c) * HALF2, 8)
    pt2[...] = dot(wt[pl.ds(wo(2), 2 * HALF2), :], zz[1])
    send(pt2.at[pl.ds(far2, HALF2), :], a2, partner).wait_recv()
    s2[...] = pt2[pl.ds(own2, HALF2), :] + a2[...]
    send(s2, b2, z1).wait_recv()
    t2[pl.ds(own2, HALF2), :] = s2[...] + b2[...]
    send(t2.at[pl.ds(own2, HALF2), :], t2.at[pl.ds(own2, HALF2), :], partner).wait_recv()
    eliminated(t2, 2)

    own3, far3 = pl.multiple_of(c * HALF3, 8), pl.multiple_of((1 - c) * HALF3, 8)
    pt3[...] = dot(wt[pl.ds(wo(3), 2 * HALF3), :], zz[2])
    send(pt3.at[pl.ds(far3, HALF3), :], a3, partner).wait_recv()
    s3[...] = pt3[pl.ds(own3, HALF3), :] + a3[...]
    send(s3, b3, z1).wait_recv()
    s3b[...] = s3[...] + b3[...]
    send(s3b, c3, z2).wait_recv()
    t3[pl.ds(own3, HALF3), :] = s3b[...] + c3[...]
    send(t3.at[pl.ds(own3, HALF3), :], t3.at[pl.ds(own3, HALF3), :], partner).wait_recv()
    eliminated(t3, 3)

    side = z // 8
    mine4 = pl.multiple_of(side * O4, 8)
    bb[pl.ds(mine4, O4), :] = dot(wt[pl.ds(wo(4), O4), :], zz[3])
    bb[pl.ds(pl.multiple_of((1 - side) * O4, 8), O4), :] = jnp.zeros((O4, R), F32)
    for level in range(5, LEVELS + 1):
        n = rows_of(level)
        bb[pl.ds(O[level], n), :] = dot(wt[pl.ds(wo(level), n), :], zz[level - 1])
    bb[pl.ds(OEND, ZROWS - OEND), :] = jnp.zeros((ZROWS - OEND, R), F32)

    own = c * ZHALF
    send(bb.at[pl.ds(pl.multiple_of((1 - c) * ZHALF, 8), ZHALF), :], rz, partner).wait_recv()
    hh[...] = bb[pl.ds(pl.multiple_of(own, 8), ZHALF), :] + rz[...]

    def part(of):
        return pl.ds(pl.multiple_of(of * PART, 8), PART)

    right = left = None
    for s in range(8):
        if s < 7:
            to = part((z + 7 - s) % NZ)
            if s == 0:
                source = hh.at[to, :]
            else:
                right.wait_recv()
                s_r[s - 1] = hh[to, :] + r_r[s - 1]
                source = s_r.at[s - 1]
            next_right = send(source, r_r.at[s], above)
        to = part((z + 8 + s) % NZ)
        if s == 0:
            source = hh.at[to, :]
        else:
            left.wait_recv()
            s_l[s - 1] = hh[to, :] + r_l[s - 1]
            source = s_l.at[s - 1]
        left = send(source, r_l.at[s], below)
        right = next_right
    right.wait_recv()
    left.wait_recv()

    def place(of):
        return pl.ds(pl.multiple_of(own + of * PART, 8), PART)

    tt[place(z), :] = hh[part(z), :] + r_r[6] + r_l[7]
    across = []
    right = left = None
    for s in range(9):
        to_right = tt.at[place((z + NZ - s) % NZ), :]
        to_left = tt.at[place((z + s) % NZ), :]
        if s > 0:
            right.wait_recv()
        if s < 8:
            right = send(to_right, to_right, above)
        if 0 < s < 8:
            left.wait_recv()
        if s < 7:
            left = send(to_left, to_left, below)
        across.append(send(to_right, to_right, partner))
        if 0 < s < 8:
            across.append(send(to_left, to_left, partner))
    for copy in across:
        copy.wait_recv()
    sent()

    halves = []
    for k in range(2):
        inverse = inv128(eye() + tt[pl.ds(k * O4, R), :])
        ki[k] = inverse
        halves.append(dot(tt[pl.ds(k * O4 + R, O4 - R), :], inverse))
    for level in range(5, LEVELS + 1):
        n = rows_of(level)
        skip = wo(level) - wo(5)
        there = pl.ds(O[level], n)
        value = tt[there, :]
        for k in range(2):
            value = value - dot(halves[k][skip:], tt[pl.ds(k * O4 + R + skip, R), :], 1, 1)
        tt[there, :] = value

    inverse5 = inv128(eye() + tt[pl.ds(O[5], R), :])
    rest5 = tt[pl.ds(O[5] + R, rows_of(6)), :]
    half5 = dot(rest5, inverse5)
    for level in range(6, LEVELS + 1):
        n = rows_of(level)
        skip = wo(level) - wo(6)
        xm[pl.ds(O[level] - O[6], n), :] = tt[pl.ds(O[level], n), :] - dot(
            half5[skip:], rest5[skip : skip + R], 1, 1
        )

    def exchanged(block, slots, rows, others, meanwhile):
        lines = pl.ds(pl.multiple_of(c * (rows // 2), 8), rows // 2)
        first = [send(block.at[lines, :], slots.at[i, lines, :], others[i]) for i in range(3)]
        meanwhile()
        second = []
        for i in range(3):
            first[i].wait_recv()
            second.append(send(slots.at[i, lines, :], slots.at[i, lines, :], partner))
        for copy in second:
            copy.wait_recv()

    def update45():
        mine = dot(ki[side], wt[pl.ds(wo(4), R), :])
        rest = pl.ds(wo(5), WUSED - wo(5))
        wt[rest, :] = wt[rest, :] - dot(
            tt[pl.ds(pl.multiple_of(mine4 + R, 8), O4 - R), :], mine
        )
        mine = dot(inverse5, wt[pl.ds(wo(5), R), :])
        rest = pl.ds(wo(6), WUSED - wo(6))
        wt[rest, :] = wt[rest, :] - dot(rest5, mine)

    exchanged(xm, xb, XROWS, xs, update45)
    u6[0] = xm[pl.ds(0, 520), :] + xb[0, pl.ds(0, 520), :]
    u6[1] = xb[1, pl.ds(0, 520), :] + xb[2, pl.ds(0, 520), :]
    halves = []
    for k in range(2):
        inverse = inv128(eye() + u6[k, pl.ds(0, R), :])
        if k == 0:
            k6[...] = inverse
        halves.append(dot(u6[k, pl.ds(R, 392), :], inverse))
    for level in range(7, LEVELS + 1):
        n = rows_of(level)
        skip = wo(level) - wo(7)
        there = pl.ds(O[level] - O[6], n)
        value = (xm[there, :] + xb[0, there, :]) + (xb[1, there, :] + xb[2, there, :])
        for k in range(2):
            value = value - dot(halves[k][skip:], u6[k, pl.ds(R + skip, R), :], 1, 1)
        s7[pl.ds(O[level] - O[7], n), :] = value
    inverse7 = inv128(eye() + s7[pl.ds(0, R), :])
    rest7 = s7[pl.ds(R, 264), :]
    half7 = dot(rest7, inverse7)
    ym[pl.ds(0, 264), :] = s7[pl.ds(392, 264), :] - dot(half7, rest7[:R], 1, 1)
    ym[pl.ds(264, 136), :] = s7[pl.ds(656, 136), :] - dot(half7[R:], rest7[R : 2 * R], 1, 1)

    exchanged(ym, yb, YROWS, ys, lambda: None)
    top = pl.ds(0, 264)
    u8 = [ym[top, :] + yb[0, top, :], yb[1, top, :] + yb[2, top, :]]
    there = pl.ds(264, 136)
    s9 = (ym[there, :] + yb[0, there, :]) + (yb[1, there, :] + yb[2, there, :])
    inverses = []
    for k in range(2):
        inverses.append(inv128(eye() + u8[k][:R]))
        rest = u8[k][R:]
        s9 = s9 - dot(dot(rest, inverses[k]), rest[:R], 1, 1)
    inverse9 = inv128(eye() + s9[:R])

    x9 = dot(s9[R:], inverse9)
    x8 = dot(u8[0][2 * R :] - dot(x9, u8[0][R : 2 * R]), inverses[0])
    right7 = s7[pl.ds(384, 8), :] - dot(x9, s7[pl.ds(256, R), :]) - dot(x8, s7[pl.ds(128, R), :])
    x7 = dot(right7, inverse7)
    right6 = u6[0, pl.ds(512, 8), :] - dot(x9, u6[0, pl.ds(384, R), :])
    right6 = right6 - dot(x8, u6[0, pl.ds(256, R), :]) - dot(x7, u6[0, pl.ds(128, R), :])
    x6 = dot(right6, k6[...])
    found = wt[pl.ds(LEVELS * R, 8), :]
    for level, value in ((9, x9), (8, x8), (7, x7), (6, x6)):
        found = found - dot(value, wt[pl.ds(wo(level), R), :])
    out[...] = jnp.transpose(found)
    sent()


def body(right_side, leaves, bases, ranks):
    v = lambda *shape: pltpu.VMEM(shape, F32)
    vmem = pl.BlockSpec(memory_space=pltpu.VMEM)
    scratch = [
        v(LEVELS, LEAF, R), v(WROWS, LEAF), v(LEAF, LEAF), v(WROWS, R), v(WROWS, R),
        v(2 * HALF2, R), v(HALF2, R), v(HALF2, R), v(HALF2, R), v(2 * HALF2, R),
        v(2 * HALF3, R), v(HALF3, R), v(HALF3, R), v(HALF3, R), v(HALF3, R), v(HALF3, R), v(2 * HALF3, R),
        v(ZROWS, R), v(ZHALF, R), v(ZHALF, R), v(6, PART, R), v(7, PART, R), v(7, PART, R), v(8, PART, R),
        v(ZROWS, R), v(2, R, R), v(XROWS, R), v(3, XROWS, R), v(2, 520, R), v(R, R), v(792, R),
        v(YROWS, R), v(3, YROWS, R),
        pltpu.SemaphoreType.DMA((72,)), pltpu.SemaphoreType.DMA((72,)),
    ]
    return pl.pallas_call(
        kernel,
        out_shape=jax.ShapeDtypeStruct((LEAF, 8), F32),
        in_specs=[pl.BlockSpec(memory_space=pltpu.SMEM), vmem, vmem, vmem],
        out_specs=vmem,
        scratch_shapes=scratch,
        compiler_params=pltpu.CompilerParams(
            collective_id=0, has_side_effects=True, vmem_limit_bytes=60 * 2**20
        ),
        name="tree",
    )(ranks, right_side, leaves, bases)


def solution(mesh):
    rows = P(("rowa", "rowb"), None)
    return jax.shard_map(
        body, mesh=mesh, in_specs=(rows, rows, P(None, ("rowa", "rowb"), None), P()),
        out_specs=rows, check_vma=False,
    )
```

```python
import jax
import jax.numpy as jnp
from jax import lax
from jax.experimental import pallas as pl
from jax.experimental.pallas import tpu as pltpu
from jax.sharding import PartitionSpec as P

F32 = jnp.float32
MESH = pl.DeviceIdType.MESH
R = 128
LEAF = 384
LEVELS = 9
NZ, NX, NY = 16, 4, 4
WROWS = LEVELS * R + 16
WUSED = LEVELS * R + 8
HALF = {2: 456, 3: 392}
PART, SUB = 112, 56
ZHALF = NZ * PART
ZROWS = 2 * ZHALF
O4 = 776
O = {5: 1552, 6: 2200, 7: 2720, 8: 3112, 9: 3376}
OEND = 3512
XROWS, YROWS = 1312, 400


def dot(a, b, ca=1, cb=0):
    dims = (((ca,), (cb,)), ((), ()))
    ah, bh = a.astype(jnp.bfloat16), b.astype(jnp.bfloat16)
    al, bl = (a - ah.astype(F32)).astype(jnp.bfloat16), (b - bh.astype(F32)).astype(jnp.bfloat16)

    def times(p, q):
        return lax.dot_general(p, q, dims, preferred_element_type=F32)

    return times(ah, bh) + (times(ah, bl) + times(al, bh))


def wo(level):
    return (level - 1) * R


def rows_of(level):
    return (LEVELS + 1 - level) * R + 8


def strip(a, lo, count, low=0):
    height = a.shape[0]
    lane = lax.broadcasted_iota(jnp.int32, (8, R), 1)
    sub = lax.broadcasted_iota(jnp.int32, (8, R), 0)
    lanes = lax.broadcasted_iota(jnp.int32, (height, R), 1)
    for step in range(0, 8 * count, 8):
        at, first = lo + step, low + step
        panel = a[first : first + 8, :]
        small = [jnp.broadcast_to(panel[:, at + j : at + j + 1], (8, R)) for j in range(8)]
        wide = [jnp.broadcast_to(a[:, at + j : at + j + 1], (height, R)) for j in range(8)]
        rows = jnp.where((lane >= at) & (lane < at + 8), jnp.where(lane - at == sub, 1.0, 0.0), panel)
        for k in range(8):
            pivot = 1.0 / small[k][k : k + 1, :]
            here = sub == k
            column = small[k]
            line = jnp.broadcast_to(rows[k : k + 1, :] * pivot, (8, R))
            rows = jnp.where(here, line, rows - column * line)
            for j in range(k + 1, 8):
                line = jnp.broadcast_to(small[j][k : k + 1, :] * pivot, (8, R))
                small[j] = jnp.where(here, line, small[j] - column * line)
        rest = jnp.where((lanes >= at) & (lanes < at + 8), 0.0, a)
        for j in range(8):
            rest = rest - wide[j] * rows[j : j + 1, :]
        parts = [part for part in (rest[:first], rows, rest[first + 8 :]) if part.shape[0]]
        a = jnp.concatenate(parts, axis=0)
    return a


def inv128(a):
    def step(_, a):
        a = strip(a, 0, 4)
        return pltpu.roll(jnp.concatenate([a[32:], a[:32]], axis=0), R - 32, 1)

    return lax.fori_loop(0, 4, step, a)


def inv_pair(a, b):
    lanes = lax.broadcasted_iota(jnp.int32, (R, R), 1)

    def step(_, pair):
        given = []
        for a in pair:
            rows = strip(a[:32], 0, 4)
            rest = jnp.where(lanes < 32, 0.0, a)[32:] - jnp.dot(
                a[32:, :32], rows, precision=lax.Precision.HIGHEST, preferred_element_type=F32
            )
            given.append(pltpu.roll(jnp.concatenate([rest, rows], axis=0), R - 32, 1))
        return tuple(given)

    return lax.fori_loop(0, 4, step, (a, b))


def eye():
    row = lax.broadcasted_iota(jnp.int32, (R, R), 0)
    column = lax.broadcasted_iota(jnp.int32, (R, R), 1)
    return jnp.where(row == column, 1.0, 0.0).astype(F32)


def flipped(value, mask):
    for bit in (1, 2, 4, 8):
        if mask & bit:
            value = value + bit - 2 * bit * ((value // bit) % 2)
    return value


def kernel(
    ranks, rhs, leaves, bases, out,
    zz, wt, dd, pt, r1, a2, b2, t2, s2, a3, b3, c3, s3, s3b, t3,
    bb, rz, hh, s_r, r_r, s_l, r_l, tt, xm, xb, u6, s7, ym, yb,
    send_sems, recv_sems,
):
    ra, rb = lax.axis_index("rowa"), lax.axis_index("rowb")
    y, x, z, c = ra // NX, ra % NX, rb // 2, rb % 2
    position = ra * (2 * NZ) + rb

    def device(y=y, x=x, z=z, c=c):
        return (y * NX + x, z * 2 + c)

    partner = device(c=1 - c)
    above, below = device(z=(z + 1) % NZ), device(z=(z + NZ - 1) % NZ)
    z1, z2 = device(z=flipped(z, 1)), device(z=flipped(z, 2))
    xs = [device(x=flipped(x, i)) for i in (1, 2, 3)]
    ys = [device(y=flipped(y, i)) for i in (1, 2, 3)]
    met = [partner, above, below, z2] + xs + ys
    barrier = pltpu.get_barrier_semaphore()
    for other in met:
        pl.semaphore_signal(barrier, inc=1, device_id=other, device_id_type=MESH)

    used = [0]
    started = []

    def send(src, dst, to):
        at = used[0]
        used[0] += 1
        copy = pltpu.make_async_remote_copy(
            src_ref=src, dst_ref=dst, send_sem=send_sems.at[at], recv_sem=recv_sems.at[at],
            device_id=to, device_id_type=MESH,
        )
        copy.start()
        started.append(copy)
        return copy

    def sent():
        for copy in started:
            copy.wait_send()
        started.clear()

    dd[...] = leaves[...]

    @pl.loop(0, 3)
    def _(_k):
        inverse = inv128(dd[:R, :R])
        line = dot(inverse, dd[:R, R:])
        column = dd[R:, :R]
        inner = dd[R:, R:] - dot(column, line)
        edge = dot(column, inverse)
        dd[: 2 * R, : 2 * R] = inner
        dd[: 2 * R, 2 * R :] = -edge
        dd[2 * R :, : 2 * R] = line
        dd[2 * R :, 2 * R :] = inverse

    lane = lax.broadcasted_iota(jnp.int32, (LEAF, R), 1)
    for level in range(1, LEVELS + 1):
        rank = ranks[2 ** (LEVELS - level) + position // 2**level - 1]
        zz[level - 1] = jnp.where(lane < rank, bases[level - 1], 0.0)

    @pl.loop(0, LEVELS)
    def _(j):
        wt[pl.ds(pl.multiple_of(j * R, R), R), :] = dot(zz[j], dd[...], 0, 0)

    wt[pl.ds(LEVELS * R, 8), :] = dot(rhs[...], dd[...])
    wt[pl.ds(WUSED, 8), :] = jnp.zeros((8, LEAF), F32)

    pl.semaphore_wait(barrier, len(met))

    def head(level):
        pt[level - 1, :R, :] = dot(wt[pl.ds(wo(level), R), :], zz[level - 1])

    def tail(level):
        count = WROWS - wo(level) - R
        pt[level - 1, pl.ds(R, count), :] = dot(wt[pl.ds(wo(level) + R, count), :], zz[level - 1])

    def eliminated(mine, total, level, between):
        first = pl.ds(wo(level + 1), R)
        wt[first, :] = wt[first, :] - dot(total[pl.ds(R, R), :], mine)
        between()
        count = WROWS - wo(level + 2)
        rest = pl.ds(wo(level + 2), count)
        wt[rest, :] = wt[rest, :] - dot(total[pl.ds(2 * R, count), :], mine)

    def pulled(inverse, level):
        return dot(inverse, wt[pl.ds(wo(level), R), :])

    count = WROWS - R
    head(1)
    ahead = send(pt.at[0, pl.ds(0, R), :], r1.at[pl.ds(0, R), :], partner)
    tail(1)
    later = send(pt.at[0, pl.ds(R, count), :], r1.at[pl.ds(R, count), :], partner)
    ahead.wait_recv()
    mine = pulled(inv128(eye() + (r1[:R, :] + pt[0, :R, :])), 1)
    later.wait_recv()
    r1[R:, :] = r1[R:, :] + pt[0, pl.ds(R, count), :]

    def spans(level):
        half = HALF[level]
        far = 1 - c
        return (
            (pl.ds(0, 64), pl.ds(pl.multiple_of(c * 64, 8), 64), pl.ds(pl.multiple_of(far * 64, 8), 64)),
            (
                pl.ds(64, half),
                pl.ds(pl.multiple_of(R + c * half, 8), half),
                pl.ds(pl.multiple_of(R + far * half, 8), half),
            ),
        )

    copies = []

    def lead(level, near):
        def run():
            head(level)
            where, _, far = spans(level)[0]
            copies.append(send(pt.at[level - 1, far, :], near.at[where, :], partner))

        return run

    def follow(level, near):
        tail(level)
        where, _, far = spans(level)[1]
        copies.append(send(pt.at[level - 1, far, :], near.at[where, :], partner))

    eliminated(mine, r1, 1, lead(2, a2))
    follow(2, a2)
    crossing = []
    for (where, own, _), copy in zip(spans(2), copies):
        copy.wait_recv()
        s2[where, :] = pt[1, own, :] + a2[where, :]
        crossing.append(send(s2.at[where, :], b2.at[where, :], z1))
    copies.clear()
    for part_of, ((where, own, _), copy) in enumerate(zip(spans(2), crossing)):
        copy.wait_recv()
        t2[own, :] = s2[where, :] + b2[where, :]
        last = send(t2.at[own, :], t2.at[own, :], partner)
        last.wait_recv()
        if part_of == 0:
            mine = pulled(inv128(eye() + t2[:R, :]), 2)

    eliminated(mine, t2, 2, lead(3, a3))
    follow(3, a3)
    crossing = []
    for (where, own, _), copy in zip(spans(3), copies):
        copy.wait_recv()
        s3[where, :] = pt[2, own, :] + a3[where, :]
        crossing.append(send(s3.at[where, :], b3.at[where, :], z1))
    farther = []
    for (where, own, _), copy in zip(spans(3), crossing):
        copy.wait_recv()
        s3b[where, :] = s3[where, :] + b3[where, :]
        farther.append(send(s3b.at[where, :], c3.at[where, :], z2))
    for part_of, ((where, own, _), copy) in enumerate(zip(spans(3), farther)):
        copy.wait_recv()
        t3[own, :] = s3b[where, :] + c3[where, :]
        last = send(t3.at[own, :], t3.at[own, :], partner)
        last.wait_recv()
        if part_of == 0:
            mine = pulled(inv128(eye() + t3[:R, :]), 3)
    eliminated(mine, t3, 3, lambda: None)

    side = z // 8
    mine4 = pl.multiple_of(side * O4, 8)
    bb[pl.ds(mine4, O4), :] = dot(wt[pl.ds(wo(4), O4), :], zz[3])
    bb[pl.ds(pl.multiple_of((1 - side) * O4, 8), O4), :] = jnp.zeros((O4, R), F32)
    for level in range(5, LEVELS + 1):
        n = rows_of(level)
        bb[pl.ds(O[level], n), :] = dot(wt[pl.ds(wo(level), n), :], zz[level - 1])
    bb[pl.ds(OEND, ZROWS - OEND), :] = jnp.zeros((ZROWS - OEND, R), F32)

    own = c * ZHALF
    other = (1 - c) * ZHALF

    def part(of, u=0, rows=PART, base=0):
        return pl.ds(pl.multiple_of(base + of * PART + u * SUB, 8), rows)

    order = [(z + 7) % NZ, (z + 8) % NZ]
    for s in range(1, 8):
        order += [(z + 7 - s) % NZ, (z + 8 + s) % NZ]
    gathered = [send(bb.at[part(of, 0, PART, other), :], rz.at[part(of), :], partner) for of in order]

    def summed(at):
        gathered[at].wait_recv()
        here = part(order[at])
        hh[here, :] = bb[part(order[at], 0, PART, own), :] + rz[here, :]

    right, left = [None, None], [None, None]
    for s in range(8):
        if s < 7:
            summed(2 * s)
        summed(2 * s + 1 if s < 7 else 15)
        for u in range(2):
            rows = pl.ds(u * SUB, SUB)
            if s < 7:
                to = part((z + 7 - s) % NZ, u, SUB)
                source = hh.at[to, :]
                if s > 0:
                    right[u].wait_recv()
                    s_r[s - 1, rows, :] = hh[to, :] + r_r[s - 1, rows, :]
                    source = s_r.at[s - 1, rows, :]
                right[u] = send(source, r_r.at[s, rows, :], above)
            to = part((z + 8 + s) % NZ, u, SUB)
            source = hh.at[to, :]
            if s > 0:
                left[u].wait_recv()
                s_l[s - 1, rows, :] = hh[to, :] + r_l[s - 1, rows, :]
                source = s_l.at[s - 1, rows, :]
            left[u] = send(source, r_l.at[s, rows, :], below)
    summed(14)
    across = []
    from_left, from_right = [None, None], [None, None]

    def place(of, u):
        return part(of % NZ, u, SUB, own)

    for u in range(2):
        rows = pl.ds(u * SUB, SUB)
        right[u].wait_recv()
        left[u].wait_recv()
        here = place(z, u)
        tt[here, :] = hh[part(z, u, SUB), :] + r_r[6, rows, :] + r_l[7, rows, :]
        from_left[u] = send(tt.at[here, :], tt.at[here, :], above)
        from_right[u] = send(tt.at[here, :], tt.at[here, :], below)
        across.append(send(tt.at[here, :], tt.at[here, :], partner))
    for s in range(1, 9):
        for u in range(2):
            from_left[u].wait_recv()
            here = place(z + NZ - s, u)
            if s < 8:
                from_left[u] = send(tt.at[here, :], tt.at[here, :], above)
            across.append(send(tt.at[here, :], tt.at[here, :], partner))
            if s < 8:
                from_right[u].wait_recv()
                here = place(z + s, u)
                if s < 7:
                    from_right[u] = send(tt.at[here, :], tt.at[here, :], below)
                across.append(send(tt.at[here, :], tt.at[here, :], partner))
    for copy in across:
        copy.wait_recv()
    sent()

    both4 = inv_pair(eye() + tt[pl.ds(0, R), :], eye() + tt[pl.ds(O4, R), :])
    halves = [dot(tt[pl.ds(k * O4 + R, O4 - R), :], both4[k]) for k in range(2)]
    for level in range(5, LEVELS + 1):
        n = rows_of(level)
        skip = wo(level) - wo(5)
        there = pl.ds(O[level], n)
        value = tt[there, :]
        for k in range(2):
            value = value - dot(halves[k][skip:], tt[pl.ds(k * O4 + R + skip, R), :], 1, 1)
        tt[there, :] = value

    inverse5 = inv128(eye() + tt[pl.ds(O[5], R), :])
    rest5 = tt[pl.ds(O[5] + R, rows_of(6)), :]
    half5 = dot(rest5, inverse5)
    for level in range(6, LEVELS + 1):
        n = rows_of(level)
        skip = wo(level) - wo(6)
        xm[pl.ds(O[level] - O[6], n), :] = tt[pl.ds(O[level], n), :] - dot(
            half5[skip:], rest5[skip : skip + R], 1, 1
        )

    def exchanged(block, slots, rows, others, meanwhile):
        half = (rows - R) // 2
        kept = []
        for start, span in ((0, 64), (R, half)):
            lines = pl.ds(pl.multiple_of(start + c * span, 8), span)
            kept.append((lines, [send(block.at[lines, :], slots.at[i, lines, :], others[i]) for i in range(3)]))
        given = None
        for lines, first in kept:
            second = []
            for i in (0, 2, 1):
                first[i].wait_recv()
                second.append(send(slots.at[i, lines, :], slots.at[i, lines, :], partner))
            for copy in second:
                copy.wait_recv()
            if given is None:
                given = meanwhile()
        return given

    def update45():
        mine = dot(jnp.where(side == 0, both4[0], both4[1]), wt[pl.ds(wo(4), R), :])
        rest = pl.ds(wo(5), WUSED - wo(5))
        wt[rest, :] = wt[rest, :] - dot(
            tt[pl.ds(pl.multiple_of(mine4 + R, 8), O4 - R), :], mine
        )
        mine = dot(inverse5, wt[pl.ds(wo(5), R), :])
        rest = pl.ds(wo(6), WUSED - wo(6))
        wt[rest, :] = wt[rest, :] - dot(rest5, mine)

    def inverses6():
        lines = pl.ds(0, R)
        pair = inv_pair(
            eye() + (xm[lines, :] + xb[0, lines, :]), eye() + (xb[1, lines, :] + xb[2, lines, :])
        )
        update45()
        return pair

    both6 = exchanged(xm, xb, XROWS, xs, inverses6)
    u6[0] = xm[pl.ds(0, 520), :] + xb[0, pl.ds(0, 520), :]
    u6[1] = xb[1, pl.ds(0, 520), :] + xb[2, pl.ds(0, 520), :]
    halves = [dot(u6[k, pl.ds(R, 392), :], both6[k]) for k in range(2)]
    for level in range(7, LEVELS + 1):
        n = rows_of(level)
        skip = wo(level) - wo(7)
        there = pl.ds(O[level] - O[6], n)
        value = (xm[there, :] + xb[0, there, :]) + (xb[1, there, :] + xb[2, there, :])
        for k in range(2):
            value = value - dot(halves[k][skip:], u6[k, pl.ds(R + skip, R), :], 1, 1)
        s7[pl.ds(O[level] - O[7], n), :] = value
    inverse7 = inv128(eye() + s7[pl.ds(0, R), :])
    rest7 = s7[pl.ds(R, 264), :]
    half7 = dot(rest7, inverse7)
    ym[pl.ds(0, 264), :] = s7[pl.ds(392, 264), :] - dot(half7, rest7[:R], 1, 1)
    ym[pl.ds(264, 136), :] = s7[pl.ds(656, 136), :] - dot(half7[R:], rest7[R : 2 * R], 1, 1)

    def inverses8():
        lines = pl.ds(0, R)
        return inv_pair(
            eye() + (ym[lines, :] + yb[0, lines, :]), eye() + (yb[1, lines, :] + yb[2, lines, :])
        )

    inverses = exchanged(ym, yb, YROWS, ys, inverses8)
    top = pl.ds(0, 264)
    u8 = [ym[top, :] + yb[0, top, :], yb[1, top, :] + yb[2, top, :]]
    there = pl.ds(264, 136)
    s9 = (ym[there, :] + yb[0, there, :]) + (yb[1, there, :] + yb[2, there, :])
    for k in range(2):
        rest = u8[k][R:]
        s9 = s9 - dot(dot(rest, inverses[k]), rest[:R], 1, 1)
    inverse9 = inv128(eye() + s9[:R])

    x9 = dot(s9[R:], inverse9)
    x8 = dot(u8[0][2 * R :] - dot(x9, u8[0][R : 2 * R]), inverses[0])
    right7 = s7[pl.ds(384, 8), :] - dot(x9, s7[pl.ds(256, R), :]) - dot(x8, s7[pl.ds(128, R), :])
    x7 = dot(right7, inverse7)
    right6 = u6[0, pl.ds(512, 8), :] - dot(x9, u6[0, pl.ds(384, R), :])
    right6 = right6 - dot(x8, u6[0, pl.ds(256, R), :]) - dot(x7, u6[0, pl.ds(128, R), :])
    x6 = dot(right6, both6[0])
    found = wt[pl.ds(LEVELS * R, 8), :]
    for level, value in ((9, x9), (8, x8), (7, x7), (6, x6)):
        found = found - dot(value, wt[pl.ds(wo(level), R), :])
    out[...] = found
    sent()


def body(right_side, leaves, bases, ranks):
    v = lambda *shape: pltpu.VMEM(shape, F32)
    vmem = pl.BlockSpec(memory_space=pltpu.VMEM)
    near2, near3 = 64 + HALF[2], 64 + HALF[3]
    scratch = [
        v(LEVELS, LEAF, R), v(WROWS, LEAF), v(LEAF, LEAF), v(3, WROWS, R), v(WROWS, R),
        v(near2, R), v(near2, R), v(2 * near2, R), v(near2, R),
        v(near3, R), v(near3, R), v(near3, R), v(near3, R), v(near3, R), v(2 * near3, R),
        v(ZROWS, R), v(ZHALF, R), v(ZHALF, R), v(6, PART, R), v(7, PART, R), v(7, PART, R), v(8, PART, R),
        v(ZROWS, R), v(XROWS, R), v(3, XROWS, R), v(2, 520, R), v(792, R),
        v(YROWS, R), v(3, YROWS, R),
        pltpu.SemaphoreType.DMA((160,)), pltpu.SemaphoreType.DMA((160,)),
    ]
    return pl.pallas_call(
        kernel,
        out_shape=jax.ShapeDtypeStruct((8, LEAF), F32),
        in_specs=[pl.BlockSpec(memory_space=pltpu.SMEM), vmem, vmem, vmem],
        out_specs=vmem,
        scratch_shapes=scratch,
        compiler_params=pltpu.CompilerParams(
            collective_id=0, has_side_effects=True, vmem_limit_bytes=60 * 2**20
        ),
        name="tree",
    )(ranks, right_side.T, leaves, bases).T


def solution(mesh):
    rows = P(("rowa", "rowb"), None)
    return jax.shard_map(
        body, mesh=mesh, in_specs=(rows, rows, P(None, ("rowa", "rowb"), None), P()),
        out_specs=rows, check_vma=False,
    )
```

```python
import jax
import jax.numpy as jnp
from jax import lax
from jax.experimental import pallas as pl
from jax.experimental.pallas import tpu as pltpu
from jax.sharding import PartitionSpec as P

F32 = jnp.float32
MESH = pl.DeviceIdType.MESH
R = 128
LEAF = 384
LEVELS = 9
NZ, NX, NY = 16, 4, 4
WROWS = LEVELS * R + 16
WUSED = LEVELS * R + 8
HALF = {2: 456, 3: 392}
PART, SUB = 112, 56
ZHALF = NZ * PART
ZROWS = 2 * ZHALF
O4 = 776
O = {5: 1552, 6: 2200, 7: 2720, 8: 3112, 9: 3376}
OEND = 3512
XROWS, YROWS = 1312, 400


def dot(a, b, ca=1, cb=0):
    dims = (((ca,), (cb,)), ((), ()))
    ah, bh = a.astype(jnp.bfloat16), b.astype(jnp.bfloat16)
    al, bl = (a - ah.astype(F32)).astype(jnp.bfloat16), (b - bh.astype(F32)).astype(jnp.bfloat16)

    def times(p, q):
        return lax.dot_general(p, q, dims, preferred_element_type=F32)

    return times(ah, bh) + (times(ah, bl) + times(al, bh))


def wo(level):
    return (level - 1) * R


def rows_of(level):
    return (LEVELS + 1 - level) * R + 8


def strip(a, lo, count, low=0):
    height = a.shape[0]
    lane = lax.broadcasted_iota(jnp.int32, (8, R), 1)
    sub = lax.broadcasted_iota(jnp.int32, (8, R), 0)
    lanes = lax.broadcasted_iota(jnp.int32, (height, R), 1)
    for step in range(0, 8 * count, 8):
        at, first = lo + step, low + step
        panel = a[first : first + 8, :]
        small = [jnp.broadcast_to(panel[:, at + j : at + j + 1], (8, R)) for j in range(8)]
        wide = [jnp.broadcast_to(a[:, at + j : at + j + 1], (height, R)) for j in range(8)]
        rows = jnp.where((lane >= at) & (lane < at + 8), jnp.where(lane - at == sub, 1.0, 0.0), panel)
        for k in range(8):
            pivot = 1.0 / small[k][k : k + 1, :]
            here = sub == k
            column = small[k]
            line = jnp.broadcast_to(rows[k : k + 1, :] * pivot, (8, R))
            rows = jnp.where(here, line, rows - column * line)
            for j in range(k + 1, 8):
                line = jnp.broadcast_to(small[j][k : k + 1, :] * pivot, (8, R))
                small[j] = jnp.where(here, line, small[j] - column * line)
        rest = jnp.where((lanes >= at) & (lanes < at + 8), 0.0, a)
        for j in range(8):
            rest = rest - wide[j] * rows[j : j + 1, :]
        parts = [part for part in (rest[:first], rows, rest[first + 8 :]) if part.shape[0]]
        a = jnp.concatenate(parts, axis=0)
    return a


def inv128(a):
    def step(_, a):
        a = strip(a, 0, 4)
        return pltpu.roll(jnp.concatenate([a[32:], a[:32]], axis=0), R - 32, 1)

    return lax.fori_loop(0, 4, step, a)


def inv_flat(a):
    return strip(a, 0, 16)


def inv_pair(a, b):
    lanes = lax.broadcasted_iota(jnp.int32, (R, R), 1)

    def step(_, pair):
        given = []
        for a in pair:
            rows = strip(a[:32], 0, 4)
            rest = jnp.where(lanes < 32, 0.0, a)[32:] - jnp.dot(
                a[32:, :32], rows, precision=lax.Precision.HIGHEST, preferred_element_type=F32
            )
            given.append(pltpu.roll(jnp.concatenate([rest, rows], axis=0), R - 32, 1))
        return tuple(given)

    return lax.fori_loop(0, 4, step, (a, b))


def eye():
    row = lax.broadcasted_iota(jnp.int32, (R, R), 0)
    column = lax.broadcasted_iota(jnp.int32, (R, R), 1)
    return jnp.where(row == column, 1.0, 0.0).astype(F32)


def flipped(value, mask):
    for bit in (1, 2, 4, 8):
        if mask & bit:
            value = value + bit - 2 * bit * ((value // bit) % 2)
    return value


def kernel(
    ranks, rhs, leaves, bases, out,
    zz, wt, dd, pt, r1, a2, b2, t2, s2, a3, b3, c3, s3, s3b, t3,
    bb, rz, hh, s_r, r_r, s_l, r_l, tt, xm, xb, u6, s7, ym, yb,
    send_sems, recv_sems,
):
    ra, rb = lax.axis_index("rowa"), lax.axis_index("rowb")
    y, x, z, c = ra // NX, ra % NX, rb // 2, rb % 2
    position = ra * (2 * NZ) + rb

    def device(y=y, x=x, z=z, c=c):
        return (y * NX + x, z * 2 + c)

    partner = device(c=1 - c)
    above, below = device(z=(z + 1) % NZ), device(z=(z + NZ - 1) % NZ)
    z1, z2 = device(z=flipped(z, 1)), device(z=flipped(z, 2))
    xs = [device(x=(x + 1) % NX), device(x=(x + NX - 1) % NX)]
    ys = [device(y=(y + 1) % NY), device(y=(y + NY - 1) % NY)]
    met = [partner, above, below, z2] + xs + ys
    barrier = pltpu.get_barrier_semaphore()
    for other in met:
        pl.semaphore_signal(barrier, inc=1, device_id=other, device_id_type=MESH)

    used = [0]
    started = []

    def send(src, dst, to):
        at = used[0]
        used[0] += 1
        copy = pltpu.make_async_remote_copy(
            src_ref=src, dst_ref=dst, send_sem=send_sems.at[at], recv_sem=recv_sems.at[at],
            device_id=to, device_id_type=MESH,
        )
        copy.start()
        started.append(copy)
        return copy

    def sent():
        for copy in started:
            copy.wait_send()
        started.clear()

    dd[...] = leaves[...]

    @pl.loop(0, 3)
    def _(_k):
        inverse = inv_flat(dd[:R, :R])
        line = dot(inverse, dd[:R, R:])
        column = dd[R:, :R]
        inner = dd[R:, R:] - dot(column, line)
        edge = dot(column, inverse)
        dd[: 2 * R, : 2 * R] = inner
        dd[: 2 * R, 2 * R :] = -edge
        dd[2 * R :, : 2 * R] = line
        dd[2 * R :, 2 * R :] = inverse

    lane = lax.broadcasted_iota(jnp.int32, (LEAF, R), 1)
    for level in range(1, LEVELS + 1):
        rank = ranks[2 ** (LEVELS - level) + position // 2**level - 1]
        zz[level - 1] = jnp.where(lane < rank, bases[level - 1], 0.0)

    wt[:R, :] = dot(zz[0], dd[...], 0, 0)
    pl.semaphore_wait(barrier, len(met))

    def head(level):
        pt[level - 1, :R, :] = dot(wt[pl.ds(wo(level), R), :], zz[level - 1])

    def tail(level):
        count = WROWS - wo(level) - R
        pt[level - 1, pl.ds(R, count), :] = dot(wt[pl.ds(wo(level) + R, count), :], zz[level - 1])

    def eliminated(mine, total, level, between):
        first = pl.ds(wo(level + 1), R)
        wt[first, :] = wt[first, :] - dot(total[pl.ds(R, R), :], mine)
        between()
        count = WROWS - wo(level + 2)
        rest = pl.ds(wo(level + 2), count)
        wt[rest, :] = wt[rest, :] - dot(total[pl.ds(2 * R, count), :], mine)

    def pulled(inverse, level):
        return dot(inverse, wt[pl.ds(wo(level), R), :])

    count = WROWS - R
    head(1)
    ahead = send(pt.at[0, pl.ds(0, R), :], r1.at[pl.ds(0, R), :], partner)

    @pl.loop(1, LEVELS)
    def _(j):
        wt[pl.ds(pl.multiple_of(j * R, R), R), :] = dot(zz[j], dd[...], 0, 0)

    wt[pl.ds(LEVELS * R, 8), :] = dot(rhs[...], dd[...])
    wt[pl.ds(WUSED, 8), :] = jnp.zeros((8, LEAF), F32)
    tail(1)
    later = send(pt.at[0, pl.ds(R, count), :], r1.at[pl.ds(R, count), :], partner)
    ahead.wait_recv()
    mine = pulled(inv128(eye() + (r1[:R, :] + pt[0, :R, :])), 1)
    later.wait_recv()
    r1[R:, :] = r1[R:, :] + pt[0, pl.ds(R, count), :]

    def spans(level):
        half = HALF[level]
        far = 1 - c
        return (
            (pl.ds(0, 64), pl.ds(pl.multiple_of(c * 64, 8), 64), pl.ds(pl.multiple_of(far * 64, 8), 64)),
            (
                pl.ds(64, half),
                pl.ds(pl.multiple_of(R + c * half, 8), half),
                pl.ds(pl.multiple_of(R + far * half, 8), half),
            ),
        )

    copies = []

    def lead(level, near):
        def run():
            head(level)
            where, _, far = spans(level)[0]
            copies.append(send(pt.at[level - 1, far, :], near.at[where, :], partner))

        return run

    def follow(level, near):
        tail(level)
        where, _, far = spans(level)[1]
        copies.append(send(pt.at[level - 1, far, :], near.at[where, :], partner))

    eliminated(mine, r1, 1, lead(2, a2))
    follow(2, a2)
    crossing = []
    for (where, own, _), copy in zip(spans(2), copies):
        copy.wait_recv()
        s2[where, :] = pt[1, own, :] + a2[where, :]
        crossing.append(send(s2.at[where, :], b2.at[where, :], z1))
    copies.clear()
    for part_of, ((where, own, _), copy) in enumerate(zip(spans(2), crossing)):
        copy.wait_recv()
        t2[own, :] = s2[where, :] + b2[where, :]
        last = send(t2.at[own, :], t2.at[own, :], partner)
        last.wait_recv()
        if part_of == 0:
            mine = pulled(inv128(eye() + t2[:R, :]), 2)

    eliminated(mine, t2, 2, lead(3, a3))
    follow(3, a3)
    crossing = []
    for (where, own, _), copy in zip(spans(3), copies):
        copy.wait_recv()
        s3[where, :] = pt[2, own, :] + a3[where, :]
        crossing.append(send(s3.at[where, :], b3.at[where, :], z1))
    farther = []
    for (where, own, _), copy in zip(spans(3), crossing):
        copy.wait_recv()
        s3b[where, :] = s3[where, :] + b3[where, :]
        farther.append(send(s3b.at[where, :], c3.at[where, :], z2))
    for part_of, ((where, own, _), copy) in enumerate(zip(spans(3), farther)):
        copy.wait_recv()
        t3[own, :] = s3b[where, :] + c3[where, :]
        last = send(t3.at[own, :], t3.at[own, :], partner)
        last.wait_recv()
        if part_of == 0:
            mine = pulled(inv128(eye() + t3[:R, :]), 3)
    eliminated(mine, t3, 3, lambda: None)

    side = z // 8
    mine4 = pl.multiple_of(side * O4, 8)
    bb[pl.ds(mine4, O4), :] = dot(wt[pl.ds(wo(4), O4), :], zz[3])
    bb[pl.ds(pl.multiple_of((1 - side) * O4, 8), O4), :] = jnp.zeros((O4, R), F32)
    for level in range(5, LEVELS + 1):
        n = rows_of(level)
        bb[pl.ds(O[level], n), :] = dot(wt[pl.ds(wo(level), n), :], zz[level - 1])
    bb[pl.ds(OEND, ZROWS - OEND), :] = jnp.zeros((ZROWS - OEND, R), F32)

    own = c * ZHALF
    other = (1 - c) * ZHALF

    def part(of, u=0, rows=PART, base=0):
        return pl.ds(pl.multiple_of(base + of * PART + u * SUB, 8), rows)

    order = [(z + 7) % NZ, (z + 8) % NZ]
    for s in range(1, 8):
        order += [(z + 7 - s) % NZ, (z + 8 + s) % NZ]
    gathered = [send(bb.at[part(of, 0, PART, other), :], rz.at[part(of), :], partner) for of in order]

    def summed(at):
        gathered[at].wait_recv()
        here = part(order[at])
        hh[here, :] = bb[part(order[at], 0, PART, own), :] + rz[here, :]

    right, left = [None, None], [None, None]
    for s in range(8):
        if s < 7:
            summed(2 * s)
        summed(2 * s + 1 if s < 7 else 15)
        for u in range(2):
            rows = pl.ds(u * SUB, SUB)
            if s < 7:
                to = part((z + 7 - s) % NZ, u, SUB)
                source = hh.at[to, :]
                if s > 0:
                    right[u].wait_recv()
                    s_r[s - 1, rows, :] = hh[to, :] + r_r[s - 1, rows, :]
                    source = s_r.at[s - 1, rows, :]
                right[u] = send(source, r_r.at[s, rows, :], above)
            to = part((z + 8 + s) % NZ, u, SUB)
            source = hh.at[to, :]
            if s > 0:
                left[u].wait_recv()
                s_l[s - 1, rows, :] = hh[to, :] + r_l[s - 1, rows, :]
                source = s_l.at[s - 1, rows, :]
            left[u] = send(source, r_l.at[s, rows, :], below)
    summed(14)
    across = []
    from_left, from_right = [None, None], [None, None]

    def place(of, u):
        return part(of % NZ, u, SUB, own)

    for u in range(2):
        rows = pl.ds(u * SUB, SUB)
        right[u].wait_recv()
        left[u].wait_recv()
        here = place(z, u)
        tt[here, :] = hh[part(z, u, SUB), :] + r_r[6, rows, :] + r_l[7, rows, :]
        from_left[u] = send(tt.at[here, :], tt.at[here, :], above)
        from_right[u] = send(tt.at[here, :], tt.at[here, :], below)
        across.append(send(tt.at[here, :], tt.at[here, :], partner))
    for s in range(1, 9):
        for u in range(2):
            from_left[u].wait_recv()
            here = place(z + NZ - s, u)
            if s < 8:
                from_left[u] = send(tt.at[here, :], tt.at[here, :], above)
            across.append(send(tt.at[here, :], tt.at[here, :], partner))
            if s < 8:
                from_right[u].wait_recv()
                here = place(z + s, u)
                if s < 7:
                    from_right[u] = send(tt.at[here, :], tt.at[here, :], below)
                across.append(send(tt.at[here, :], tt.at[here, :], partner))
    for copy in across:
        copy.wait_recv()
    sent()

    both4 = inv_pair(eye() + tt[pl.ds(0, R), :], eye() + tt[pl.ds(O4, R), :])
    halves = [dot(tt[pl.ds(k * O4 + R, O4 - R), :], both4[k]) for k in range(2)]
    for level in range(5, LEVELS + 1):
        n = rows_of(level)
        skip = wo(level) - wo(5)
        there = pl.ds(O[level], n)
        value = tt[there, :]
        for k in range(2):
            value = value - dot(halves[k][skip:], tt[pl.ds(k * O4 + R + skip, R), :], 1, 1)
        tt[there, :] = value

    inverse5 = inv_flat(eye() + tt[pl.ds(O[5], R), :])
    rest5 = tt[pl.ds(O[5] + R, rows_of(6)), :]
    xm[:R, :] = tt[pl.ds(O[6], R), :] - dot(dot(rest5[:R], inverse5), rest5[:R], 1, 1)

    def prepared5():
        half5 = dot(rest5, inverse5)
        for level in range(6, LEVELS + 1):
            skip = wo(level) - wo(6)
            first = R if level == 6 else 0
            n = rows_of(level) - first
            xm[pl.ds(O[level] - O[6] + first, n), :] = tt[pl.ds(O[level] + first, n), :] - dot(
                half5[skip + first :], rest5[skip : skip + R], 1, 1
            )

    def exchanged(block, slots, rows, others, prepare, invert, fill):
        after, before = others
        half = (rows - R) // 2
        cut = (half // 16) * 8
        streams = []
        for start, span, piece in ((0, 64, 32), (R, half, cut)):
            base = start + c * span
            lines = pl.ds(pl.multiple_of(base, 8), span)
            one = pl.ds(pl.multiple_of(base, 8), piece)
            two = pl.ds(pl.multiple_of(base + piece, 8), span - piece)
            up = send(block.at[lines, :], slots.at[0, lines, :], after)
            down = send(block.at[lines, :], slots.at[1, lines, :], before)
            streams.append((lines, one, two, up, down))
            if start == 0:
                prepare()
        inverses = None
        for lines, one, two, up, down in streams:
            up.wait_recv()
            on = [send(slots.at[0, one, :], slots.at[2, one, :], after)]
            shared = [send(slots.at[0, lines, :], slots.at[0, lines, :], partner)]
            down.wait_recv()
            on.append(send(slots.at[1, two, :], slots.at[2, two, :], before))
            shared.append(send(slots.at[1, lines, :], slots.at[1, lines, :], partner))
            if inverses is not None:
                fill()
            for copy, where in zip(on, (one, two)):
                copy.wait_recv()
                shared.append(send(slots.at[2, where, :], slots.at[2, where, :], partner))
            for copy in shared:
                copy.wait_recv()
            if inverses is None:
                inverses = invert()
        return inverses

    def update45():
        mine = dot(jnp.where(side == 0, both4[0], both4[1]), wt[pl.ds(wo(4), R), :])
        rest = pl.ds(wo(5), WUSED - wo(5))
        wt[rest, :] = wt[rest, :] - dot(
            tt[pl.ds(pl.multiple_of(mine4 + R, 8), O4 - R), :], mine
        )
        mine = dot(inverse5, wt[pl.ds(wo(5), R), :])
        rest = pl.ds(wo(6), WUSED - wo(6))
        wt[rest, :] = wt[rest, :] - dot(rest5, mine)

    xmate, xnear = 1 - x % 2, x % 2

    def inverses6():
        lines = pl.ds(0, R)
        return inv_pair(
            eye() + (xm[lines, :] + xb[xmate, lines, :]), eye() + (xb[xnear, lines, :] + xb[2, lines, :])
        )

    both6 = exchanged(xm, xb, XROWS, xs, prepared5, inverses6, update45)
    u6[0] = xm[pl.ds(0, 520), :] + xb[xmate, pl.ds(0, 520), :]
    u6[1] = xb[xnear, pl.ds(0, 520), :] + xb[2, pl.ds(0, 520), :]
    halves = [dot(u6[k, pl.ds(R, 392), :], both6[k]) for k in range(2)]
    for level in range(7, LEVELS + 1):
        n = rows_of(level)
        skip = wo(level) - wo(7)
        there = pl.ds(O[level] - O[6], n)
        value = (xm[there, :] + xb[xmate, there, :]) + (xb[xnear, there, :] + xb[2, there, :])
        for k in range(2):
            value = value - dot(halves[k][skip:], u6[k, pl.ds(R + skip, R), :], 1, 1)
        s7[pl.ds(O[level] - O[7], n), :] = value
    inverse7 = inv_flat(eye() + s7[pl.ds(0, R), :])
    rest7 = s7[pl.ds(R, 264), :]
    half7 = dot(rest7[:R], inverse7)
    ym[:R, :] = s7[pl.ds(392, R), :] - dot(half7, rest7[:R], 1, 1)

    def prepared7():
        half7 = dot(rest7[R:], inverse7)
        ym[pl.ds(R, 136), :] = s7[pl.ds(392 + R, 136), :] - dot(half7, rest7[:R], 1, 1)
        ym[pl.ds(264, 136), :] = s7[pl.ds(656, 136), :] - dot(half7, rest7[R : 2 * R], 1, 1)


    ymate, ynear = 1 - y % 2, y % 2

    def inverses8():
        lines = pl.ds(0, R)
        return inv_pair(
            eye() + (ym[lines, :] + yb[ymate, lines, :]), eye() + (yb[ynear, lines, :] + yb[2, lines, :])
        )

    inverses = exchanged(ym, yb, YROWS, ys, prepared7, inverses8, lambda: None)
    top = pl.ds(0, 264)
    u8 = [ym[top, :] + yb[ymate, top, :], yb[ynear, top, :] + yb[2, top, :]]
    there = pl.ds(264, 136)
    s9 = (ym[there, :] + yb[ymate, there, :]) + (yb[ynear, there, :] + yb[2, there, :])
    for k in range(2):
        rest = u8[k][R:]
        s9 = s9 - dot(dot(rest, inverses[k]), rest[:R], 1, 1)
    inverse9 = inv_flat(eye() + s9[:R])

    x9 = dot(s9[R:], inverse9)
    x8 = dot(u8[0][2 * R :] - dot(x9, u8[0][R : 2 * R]), inverses[0])
    right7 = s7[pl.ds(384, 8), :] - dot(x9, s7[pl.ds(256, R), :]) - dot(x8, s7[pl.ds(128, R), :])
    x7 = dot(right7, inverse7)
    right6 = u6[0, pl.ds(512, 8), :] - dot(x9, u6[0, pl.ds(384, R), :])
    right6 = right6 - dot(x8, u6[0, pl.ds(256, R), :]) - dot(x7, u6[0, pl.ds(128, R), :])
    x6 = dot(right6, both6[0])
    found = wt[pl.ds(LEVELS * R, 8), :]
    for level, value in ((9, x9), (8, x8), (7, x7), (6, x6)):
        found = found - dot(value, wt[pl.ds(wo(level), R), :])
    out[...] = found
    sent()


def body(right_side, leaves, bases, ranks):
    v = lambda *shape: pltpu.VMEM(shape, F32)
    vmem = pl.BlockSpec(memory_space=pltpu.VMEM)
    near2, near3 = 64 + HALF[2], 64 + HALF[3]
    scratch = [
        v(LEVELS, LEAF, R), v(WROWS, LEAF), v(LEAF, LEAF), v(3, WROWS, R), v(WROWS, R),
        v(near2, R), v(near2, R), v(2 * near2, R), v(near2, R),
        v(near3, R), v(near3, R), v(near3, R), v(near3, R), v(near3, R), v(2 * near3, R),
        v(ZROWS, R), v(ZHALF, R), v(ZHALF, R), v(6, PART, R), v(7, PART, R), v(7, PART, R), v(8, PART, R),
        v(ZROWS, R), v(XROWS, R), v(3, XROWS, R), v(2, 520, R), v(792, R),
        v(YROWS, R), v(3, YROWS, R),
        pltpu.SemaphoreType.DMA((160,)), pltpu.SemaphoreType.DMA((160,)),
    ]
    return pl.pallas_call(
        kernel,
        out_shape=jax.ShapeDtypeStruct((8, LEAF), F32),
        in_specs=[pl.BlockSpec(memory_space=pltpu.SMEM), vmem, vmem, vmem],
        out_specs=vmem,
        scratch_shapes=scratch,
        compiler_params=pltpu.CompilerParams(
            collective_id=0, has_side_effects=True, vmem_limit_bytes=60 * 2**20
        ),
        name="tree",
    )(ranks, right_side.T, leaves, bases).T


def solution(mesh):
    rows = P(("rowa", "rowb"), None)
    return jax.shard_map(
        body, mesh=mesh, in_specs=(rows, rows, P(None, ("rowa", "rowb"), None), P()),
        out_specs=rows, check_vma=False,
    )
```

```python
import jax
import jax.numpy as jnp
from jax import lax
from jax.experimental import pallas as pl
from jax.experimental.pallas import tpu as pltpu
from jax.sharding import PartitionSpec as P

F32 = jnp.float32
MESH = pl.DeviceIdType.MESH
R = 128
LEAF = 384
LEVELS = 9
NZ, NX, NY = 16, 4, 4
WROWS = LEVELS * R + 16
WUSED = LEVELS * R + 8
HALF = {2: 456, 3: 392}
PART, SUB = 112, 56
ZHALF = NZ * PART
ZROWS = 2 * ZHALF
O4 = 776
O = {5: 1552, 6: 2200, 7: 2720, 8: 3112, 9: 3376}
OEND = 3512
XROWS, YROWS = 1312, 400


def dot(a, b, ca=1, cb=0):
    dims = (((ca,), (cb,)), ((), ()))
    ah, bh = a.astype(jnp.bfloat16), b.astype(jnp.bfloat16)
    al, bl = (a - ah.astype(F32)).astype(jnp.bfloat16), (b - bh.astype(F32)).astype(jnp.bfloat16)

    def times(p, q):
        return lax.dot_general(p, q, dims, preferred_element_type=F32)

    return times(ah, bh) + (times(ah, bl) + times(al, bh))


def wo(level):
    return (level - 1) * R


def rows_of(level):
    return (LEVELS + 1 - level) * R + 8


def strip(a, lo, count, low=0):
    height = a.shape[0]
    lane = lax.broadcasted_iota(jnp.int32, (8, R), 1)
    sub = lax.broadcasted_iota(jnp.int32, (8, R), 0)
    lanes = lax.broadcasted_iota(jnp.int32, (height, R), 1)
    for step in range(0, 8 * count, 8):
        at, first = lo + step, low + step
        panel = a[first : first + 8, :]
        small = [jnp.broadcast_to(panel[:, at + j : at + j + 1], (8, R)) for j in range(8)]
        wide = [jnp.broadcast_to(a[:, at + j : at + j + 1], (height, R)) for j in range(8)]
        rows = jnp.where((lane >= at) & (lane < at + 8), jnp.where(lane - at == sub, 1.0, 0.0), panel)
        for k in range(8):
            pivot = 1.0 / small[k][k : k + 1, :]
            here = sub == k
            column = small[k]
            line = jnp.broadcast_to(rows[k : k + 1, :] * pivot, (8, R))
            rows = jnp.where(here, line, rows - column * line)
            for j in range(k + 1, 8):
                line = jnp.broadcast_to(small[j][k : k + 1, :] * pivot, (8, R))
                small[j] = jnp.where(here, line, small[j] - column * line)
        rest = jnp.where((lanes >= at) & (lanes < at + 8), 0.0, a)
        for j in range(8):
            rest = rest - wide[j] * rows[j : j + 1, :]
        parts = [part for part in (rest[:first], rows, rest[first + 8 :]) if part.shape[0]]
        a = jnp.concatenate(parts, axis=0)
    return a


def inv128(a):
    def step(_, a):
        a = strip(a, 0, 4)
        return pltpu.roll(jnp.concatenate([a[32:], a[:32]], axis=0), R - 32, 1)

    return lax.fori_loop(0, 4, step, a)


def inv_flat(a):
    return strip(a, 0, 16)


def inv_pair(a, b):
    lanes = lax.broadcasted_iota(jnp.int32, (R, R), 1)

    def step(_, pair):
        given = []
        for a in pair:
            rows = strip(a[:32], 0, 4)
            rest = jnp.where(lanes < 32, 0.0, a)[32:] - jnp.dot(
                a[32:, :32], rows, precision=lax.Precision.HIGHEST, preferred_element_type=F32
            )
            given.append(pltpu.roll(jnp.concatenate([rest, rows], axis=0), R - 32, 1))
        return tuple(given)

    return lax.fori_loop(0, 4, step, (a, b))


def eye():
    row = lax.broadcasted_iota(jnp.int32, (R, R), 0)
    column = lax.broadcasted_iota(jnp.int32, (R, R), 1)
    return jnp.where(row == column, 1.0, 0.0).astype(F32)


def flipped(value, mask):
    for bit in (1, 2, 4, 8):
        if mask & bit:
            value = value + bit - 2 * bit * ((value // bit) % 2)
    return value


def kernel(
    ranks, rhs, leaves, bases, out,
    zz, wt, dd, pt, r1, a2, b2, t2, s2, a3, b3, c3, s3, s3b, t3,
    bb, rz, hh, s_r, r_r, s_l, r_l, tt, xm, xb, u6, s7, ym, yb,
    send_sems, recv_sems,
):
    ra, rb = lax.axis_index("rowa"), lax.axis_index("rowb")
    y, x, z, c = ra // NX, ra % NX, rb // 2, rb % 2
    position = ra * (2 * NZ) + rb

    def device(y=y, x=x, z=z, c=c):
        return (y * NX + x, z * 2 + c)

    partner = device(c=1 - c)
    above, below = device(z=(z + 1) % NZ), device(z=(z + NZ - 1) % NZ)
    z1, z2 = device(z=flipped(z, 1)), device(z=flipped(z, 2))
    xs = [device(x=flipped(x, i)) for i in (1, 2, 3)]
    ys = [device(y=flipped(y, i)) for i in (1, 2, 3)]
    met = [partner, above, below, z2] + xs + ys
    barrier = pltpu.get_barrier_semaphore()
    for other in met:
        pl.semaphore_signal(barrier, inc=1, device_id=other, device_id_type=MESH)

    used = [0]
    started = []

    def send(src, dst, to):
        at = used[0]
        used[0] += 1
        copy = pltpu.make_async_remote_copy(
            src_ref=src, dst_ref=dst, send_sem=send_sems.at[at], recv_sem=recv_sems.at[at],
            device_id=to, device_id_type=MESH,
        )
        copy.start()
        started.append(copy)
        return copy

    def sent():
        for copy in started:
            copy.wait_send()
        started.clear()

    dd[...] = leaves[...]

    @pl.loop(0, 3)
    def _(_k):
        inverse = inv_flat(dd[:R, :R])
        line = dot(inverse, dd[:R, R:])
        column = dd[R:, :R]
        inner = dd[R:, R:] - dot(column, line)
        edge = dot(column, inverse)
        dd[: 2 * R, : 2 * R] = inner
        dd[: 2 * R, 2 * R :] = -edge
        dd[2 * R :, : 2 * R] = line
        dd[2 * R :, 2 * R :] = inverse

    lane = lax.broadcasted_iota(jnp.int32, (LEAF, R), 1)
    for level in range(1, LEVELS + 1):
        rank = ranks[2 ** (LEVELS - level) + position // 2**level - 1]
        zz[level - 1] = jnp.where(lane < rank, bases[level - 1], 0.0)

    wt[:R, :] = dot(zz[0], dd[...], 0, 0)
    pl.semaphore_wait(barrier, len(met))

    def head(level):
        pt[level - 1, :R, :] = dot(wt[pl.ds(wo(level), R), :], zz[level - 1])

    def tail(level):
        count = WROWS - wo(level) - R
        pt[level - 1, pl.ds(R, count), :] = dot(wt[pl.ds(wo(level) + R, count), :], zz[level - 1])

    def eliminated(mine, total, level, between):
        first = pl.ds(wo(level + 1), R)
        wt[first, :] = wt[first, :] - dot(total[pl.ds(R, R), :], mine)
        between()
        count = WROWS - wo(level + 2)
        rest = pl.ds(wo(level + 2), count)
        wt[rest, :] = wt[rest, :] - dot(total[pl.ds(2 * R, count), :], mine)

    def pulled(inverse, level):
        return dot(inverse, wt[pl.ds(wo(level), R), :])

    count = WROWS - R
    head(1)
    ahead = send(pt.at[0, pl.ds(0, R), :], r1.at[pl.ds(0, R), :], partner)

    @pl.loop(1, LEVELS)
    def _(j):
        wt[pl.ds(pl.multiple_of(j * R, R), R), :] = dot(zz[j], dd[...], 0, 0)

    wt[pl.ds(LEVELS * R, 8), :] = dot(rhs[...], dd[...])
    wt[pl.ds(WUSED, 8), :] = jnp.zeros((8, LEAF), F32)
    tail(1)
    later = send(pt.at[0, pl.ds(R, count), :], r1.at[pl.ds(R, count), :], partner)
    ahead.wait_recv()
    mine = pulled(inv_flat(eye() + (r1[:R, :] + pt[0, :R, :])), 1)
    later.wait_recv()
    r1[R:, :] = r1[R:, :] + pt[0, pl.ds(R, count), :]

    def spans(level):
        half = HALF[level]
        first = (half // 16) * 8 + 8
        far = 1 - c
        given = []
        for near, start, stride, rows in (
            (0, 0, 64, 64), (64, R, half, first), (64 + first, R + first, half, half - first)
        ):
            own = pl.ds(pl.multiple_of(start + c * stride, 8), rows)
            given.append((pl.ds(near, rows), own, pl.ds(pl.multiple_of(start + far * stride, 8), rows)))
        return given

    copies = []

    def lead(level, near):
        def run():
            head(level)
            where, _, far = spans(level)[0]
            copies.append(send(pt.at[level - 1, far, :], near.at[where, :], partner))

        return run

    def follow(level, near):
        tail(level)
        for where, _, far in spans(level)[1:]:
            copies.append(send(pt.at[level - 1, far, :], near.at[where, :], partner))

    eliminated(mine, r1, 1, lead(2, a2))
    follow(2, a2)
    crossing = []
    for (where, own, _), copy in zip(spans(2), copies):
        copy.wait_recv()
        s2[where, :] = pt[1, own, :] + a2[where, :]
        crossing.append(send(s2.at[where, :], b2.at[where, :], z1))
    copies.clear()
    last = []
    for part_of, ((where, own, _), copy) in enumerate(zip(spans(2), crossing)):
        copy.wait_recv()
        t2[own, :] = s2[where, :] + b2[where, :]
        last.append(send(t2.at[own, :], t2.at[own, :], partner))
        if part_of == 0:
            last.pop().wait_recv()
            mine = pulled(inv128(eye() + t2[:R, :]), 2)
    for copy in last:
        copy.wait_recv()

    eliminated(mine, t2, 2, lead(3, a3))
    follow(3, a3)
    crossing = []
    for (where, own, _), copy in zip(spans(3), copies):
        copy.wait_recv()
        s3[where, :] = pt[2, own, :] + a3[where, :]
        crossing.append(send(s3.at[where, :], b3.at[where, :], z1))
    farther = []
    for (where, own, _), copy in zip(spans(3), crossing):
        copy.wait_recv()
        s3b[where, :] = s3[where, :] + b3[where, :]
        farther.append(send(s3b.at[where, :], c3.at[where, :], z2))
    last = []
    for part_of, ((where, own, _), copy) in enumerate(zip(spans(3), farther)):
        copy.wait_recv()
        t3[own, :] = s3b[where, :] + c3[where, :]
        last.append(send(t3.at[own, :], t3.at[own, :], partner))
        if part_of == 0:
            last.pop().wait_recv()
            mine = pulled(inv128(eye() + t3[:R, :]), 3)
    for copy in last:
        copy.wait_recv()
    eliminated(mine, t3, 3, lambda: None)

    side = z // 8
    mine4 = pl.multiple_of(side * O4, 8)
    bb[pl.ds(mine4, O4), :] = dot(wt[pl.ds(wo(4), O4), :], zz[3])
    bb[pl.ds(pl.multiple_of((1 - side) * O4, 8), O4), :] = jnp.zeros((O4, R), F32)
    for level in range(5, LEVELS + 1):
        n = rows_of(level)
        bb[pl.ds(O[level], n), :] = dot(wt[pl.ds(wo(level), n), :], zz[level - 1])
    bb[pl.ds(OEND, ZROWS - OEND), :] = jnp.zeros((ZROWS - OEND, R), F32)

    own = c * ZHALF
    other = (1 - c) * ZHALF

    def part(of, u=0, rows=PART, base=0):
        return pl.ds(pl.multiple_of(base + of * PART + u * SUB, 8), rows)

    order = [(z + 7) % NZ, (z + 8) % NZ]
    for s in range(1, 8):
        order += [(z + 7 - s) % NZ, (z + 8 + s) % NZ]
    gathered = [send(bb.at[part(of, 0, PART, other), :], rz.at[part(of), :], partner) for of in order]

    def summed(at):
        gathered[at].wait_recv()
        here = part(order[at])
        hh[here, :] = bb[part(order[at], 0, PART, own), :] + rz[here, :]

    right, left = [None, None], [None, None]
    for s in range(8):
        if s < 7:
            summed(2 * s)
        summed(2 * s + 1 if s < 7 else 15)
        for u in range(2):
            rows = pl.ds(u * SUB, SUB)
            if s < 7:
                to = part((z + 7 - s) % NZ, u, SUB)
                source = hh.at[to, :]
                if s > 0:
                    right[u].wait_recv()
                    s_r[s - 1, rows, :] = hh[to, :] + r_r[s - 1, rows, :]
                    source = s_r.at[s - 1, rows, :]
                right[u] = send(source, r_r.at[s, rows, :], above)
            to = part((z + 8 + s) % NZ, u, SUB)
            source = hh.at[to, :]
            if s > 0:
                left[u].wait_recv()
                s_l[s - 1, rows, :] = hh[to, :] + r_l[s - 1, rows, :]
                source = s_l.at[s - 1, rows, :]
            left[u] = send(source, r_l.at[s, rows, :], below)
    summed(14)
    across = []
    from_left, from_right = [None, None], [None, None]

    def place(of, u):
        return part(of % NZ, u, SUB, own)

    for u in range(2):
        rows = pl.ds(u * SUB, SUB)
        right[u].wait_recv()
        left[u].wait_recv()
        here = place(z, u)
        tt[here, :] = hh[part(z, u, SUB), :] + r_r[6, rows, :] + r_l[7, rows, :]
        from_left[u] = send(tt.at[here, :], tt.at[here, :], above)
        from_right[u] = send(tt.at[here, :], tt.at[here, :], below)
        across.append(send(tt.at[here, :], tt.at[here, :], partner))
    for s in range(1, 9):
        for u in range(2):
            from_left[u].wait_recv()
            here = place(z + NZ - s, u)
            if s < 8:
                from_left[u] = send(tt.at[here, :], tt.at[here, :], above)
            across.append(send(tt.at[here, :], tt.at[here, :], partner))
            if s < 8:
                from_right[u].wait_recv()
                here = place(z + s, u)
                if s < 7:
                    from_right[u] = send(tt.at[here, :], tt.at[here, :], below)
                across.append(send(tt.at[here, :], tt.at[here, :], partner))
    for copy in across:
        copy.wait_recv()
    sent()

    both4 = inv_pair(eye() + tt[pl.ds(0, R), :], eye() + tt[pl.ds(O4, R), :])
    halves = [dot(tt[pl.ds(k * O4 + R, O4 - R), :], both4[k]) for k in range(2)]
    for level in range(5, LEVELS + 1):
        n = rows_of(level)
        skip = wo(level) - wo(5)
        there = pl.ds(O[level], n)
        value = tt[there, :]
        for k in range(2):
            value = value - dot(halves[k][skip:], tt[pl.ds(k * O4 + R + skip, R), :], 1, 1)
        tt[there, :] = value

    inverse5 = inv_flat(eye() + tt[pl.ds(O[5], R), :])
    rest5 = tt[pl.ds(O[5] + R, rows_of(6)), :]
    xm[:R, :] = tt[pl.ds(O[6], R), :] - dot(dot(rest5[:R], inverse5), rest5[:R], 1, 1)

    def prepared5():
        half5 = dot(rest5, inverse5)
        for level in range(6, LEVELS + 1):
            skip = wo(level) - wo(6)
            first = R if level == 6 else 0
            n = rows_of(level) - first
            xm[pl.ds(O[level] - O[6] + first, n), :] = tt[pl.ds(O[level] + first, n), :] - dot(
                half5[skip + first :], rest5[skip : skip + R], 1, 1
            )

    def exchanged(block, slots, rows, others, prepare, invert, fill):
        half = (rows - R) // 2
        streams = []
        for start, span in ((0, 64), (R, half)):
            lines = pl.ds(pl.multiple_of(start + c * span, 8), span)
            streams.append((lines, [send(block.at[lines, :], slots.at[i, lines, :], others[i]) for i in range(3)]))
            if start == 0:
                prepare()
        inverses = None
        for lines, first in streams:
            if inverses is not None:
                fill()
            shared = []
            for i in (0, 2, 1):
                first[i].wait_recv()
                shared.append(send(slots.at[i, lines, :], slots.at[i, lines, :], partner))
            for copy in shared:
                copy.wait_recv()
            if inverses is None:
                inverses = invert()
        return inverses

    def update45():
        mine = dot(jnp.where(side == 0, both4[0], both4[1]), wt[pl.ds(wo(4), R), :])
        rest = pl.ds(wo(5), WUSED - wo(5))
        wt[rest, :] = wt[rest, :] - dot(
            tt[pl.ds(pl.multiple_of(mine4 + R, 8), O4 - R), :], mine
        )
        mine = dot(inverse5, wt[pl.ds(wo(5), R), :])
        rest = pl.ds(wo(6), WUSED - wo(6))
        wt[rest, :] = wt[rest, :] - dot(rest5, mine)

    def inverses6():
        lines = pl.ds(0, R)
        return inv_pair(
            eye() + (xm[lines, :] + xb[0, lines, :]), eye() + (xb[1, lines, :] + xb[2, lines, :])
        )

    both6 = exchanged(xm, xb, XROWS, xs, prepared5, inverses6, update45)
    u6[0] = xm[pl.ds(0, 520), :] + xb[0, pl.ds(0, 520), :]
    u6[1] = xb[1, pl.ds(0, 520), :] + xb[2, pl.ds(0, 520), :]
    halves = [dot(u6[k, pl.ds(R, 392), :], both6[k]) for k in range(2)]
    for level in range(7, LEVELS + 1):
        n = rows_of(level)
        skip = wo(level) - wo(7)
        there = pl.ds(O[level] - O[6], n)
        value = (xm[there, :] + xb[0, there, :]) + (xb[1, there, :] + xb[2, there, :])
        for k in range(2):
            value = value - dot(halves[k][skip:], u6[k, pl.ds(R + skip, R), :], 1, 1)
        s7[pl.ds(O[level] - O[7], n), :] = value
    inverse7 = inv_flat(eye() + s7[pl.ds(0, R), :])
    rest7 = s7[pl.ds(R, 264), :]
    half7 = dot(rest7[:R], inverse7)
    ym[:R, :] = s7[pl.ds(392, R), :] - dot(half7, rest7[:R], 1, 1)

    def prepared7():
        half7 = dot(rest7[R:], inverse7)
        ym[pl.ds(R, 136), :] = s7[pl.ds(392 + R, 136), :] - dot(half7, rest7[:R], 1, 1)
        ym[pl.ds(264, 136), :] = s7[pl.ds(656, 136), :] - dot(half7, rest7[R : 2 * R], 1, 1)


    def inverses8():
        lines = pl.ds(0, R)
        return inv_pair(
            eye() + (ym[lines, :] + yb[0, lines, :]), eye() + (yb[1, lines, :] + yb[2, lines, :])
        )

    inverses = exchanged(ym, yb, YROWS, ys, prepared7, inverses8, lambda: None)
    top = pl.ds(0, 264)
    u8 = [ym[top, :] + yb[0, top, :], yb[1, top, :] + yb[2, top, :]]
    there = pl.ds(264, 136)
    s9 = (ym[there, :] + yb[0, there, :]) + (yb[1, there, :] + yb[2, there, :])
    for k in range(2):
        rest = u8[k][R:]
        s9 = s9 - dot(dot(rest, inverses[k]), rest[:R], 1, 1)
    inverse9 = inv_flat(eye() + s9[:R])

    x9 = dot(s9[R:], inverse9)
    x8 = dot(u8[0][2 * R :] - dot(x9, u8[0][R : 2 * R]), inverses[0])
    right7 = s7[pl.ds(384, 8), :] - dot(x9, s7[pl.ds(256, R), :]) - dot(x8, s7[pl.ds(128, R), :])
    x7 = dot(right7, inverse7)
    right6 = u6[0, pl.ds(512, 8), :] - dot(x9, u6[0, pl.ds(384, R), :])
    right6 = right6 - dot(x8, u6[0, pl.ds(256, R), :]) - dot(x7, u6[0, pl.ds(128, R), :])
    x6 = dot(right6, both6[0])
    found = wt[pl.ds(LEVELS * R, 8), :]
    for level, value in ((9, x9), (8, x8), (7, x7), (6, x6)):
        found = found - dot(value, wt[pl.ds(wo(level), R), :])
    out[...] = found
    sent()


def body(right_side, leaves, bases, ranks):
    v = lambda *shape: pltpu.VMEM(shape, F32)
    vmem = pl.BlockSpec(memory_space=pltpu.VMEM)
    near2, near3 = 64 + HALF[2], 64 + HALF[3]
    scratch = [
        v(LEVELS, LEAF, R), v(WROWS, LEAF), v(LEAF, LEAF), v(3, WROWS, R), v(WROWS, R),
        v(near2, R), v(near2, R), v(2 * near2, R), v(near2, R),
        v(near3, R), v(near3, R), v(near3, R), v(near3, R), v(near3, R), v(2 * near3, R),
        v(ZROWS, R), v(ZHALF, R), v(ZHALF, R), v(6, PART, R), v(7, PART, R), v(7, PART, R), v(8, PART, R),
        v(ZROWS, R), v(XROWS, R), v(3, XROWS, R), v(2, 520, R), v(792, R),
        v(YROWS, R), v(3, YROWS, R),
        pltpu.SemaphoreType.DMA((160,)), pltpu.SemaphoreType.DMA((160,)),
    ]
    return pl.pallas_call(
        kernel,
        out_shape=jax.ShapeDtypeStruct((8, LEAF), F32),
        in_specs=[pl.BlockSpec(memory_space=pltpu.SMEM), vmem, vmem, vmem],
        out_specs=vmem,
        scratch_shapes=scratch,
        compiler_params=pltpu.CompilerParams(
            collective_id=0, has_side_effects=True, vmem_limit_bytes=60 * 2**20
        ),
        name="tree",
    )(ranks, right_side.T, leaves, bases).T


def solution(mesh):
    rows = P(("rowa", "rowb"), None)
    return jax.shard_map(
        body, mesh=mesh, in_specs=(rows, rows, P(None, ("rowa", "rowb"), None), P()),
        out_specs=rows, check_vma=False,
    )
```
